32 devices in a mesh: ctx: 8 (over z, x), ch: 4 (over y, core).
Axes of the slice: x: 2, y: 2, z: 4, core: 2. Of those that a mesh axis runs over, the one named last changes fastest.
Arguments:
- short_conv_input: bfloat16 [1024, 1024], P('ctx', 'ch'), may hold values from -6 to 6
- out_gate: bfloat16 [1024, 1024], P('ctx', 'ch'), may hold values from -6 to 6
- in_gate: bfloat16 [1024, 1024], P('ctx', 'ch'), may hold values from -6 to 6
- out_cotangent: bfloat16 [1024, 1024], P('ctx', 'ch'), may hold values from -6 to 6
- mr_filter: bfloat16 [128, 64], P(None, 'ch'), may hold values from -0.5 to 0.5
- residues: float32 [16, 1024], P(None, ('ch', 'ctx')), may hold values from -5 to 5
- rates: float32 [16, 1024], P(None, ('ch', 'ctx')), may hold values from 0.0009765625 to 0.03
Outputs:
- input_grad: bfloat16 [1024, 1024], P('ctx', 'ch')
- out_gate_grad: bfloat16 [1024, 1024], P('ctx', 'ch')
- in_gate_grad: bfloat16 [1024, 1024], P('ctx', 'ch')
- filter_grad: float32 [128, 64], P(None, 'ch')
- residue_grad: float32 [16, 1024], P(None, ('ch', 'ctx'))
- rate_grad: float32 [16, 1024], P(None, ('ch', 'ctx'))
The draws below stay inside these ranges and needn't reach their ends.
All inputs are finite; a program needn't handle non-finite values.
Results may differ from the reference program's by a relative error of at most 0.013.
Values may be sent and summed in bfloat16 or wider, within the bound.
A program may use at most 64 MiB of HBM per device.

```python
import math
import jax
import jax.numpy as jnp
from jax import lax

CHANNELS = 1024
FILTER_TAPS = 128
GROUP = 16
MODES = 16
TOKENS = 1024
GROUPS = 64


def level_of(stream_key, extent, shards, smallest, high):
    gain, own = 1.0, jax.random.fold_in(stream_key, 6)
    for axis_at, blocks in shards:
        heights = jnp.exp(jax.random.uniform(jax.random.fold_in(own, axis_at), (blocks,), jnp.float32, smallest / len(shards), high / len(shards)))
        gain = gain * jnp.repeat(heights, extent[axis_at] // blocks).reshape([-1 if axis == axis_at else 1 for axis in range(len(extent))])
    return gain


def centred(own_key, dims, spread, bound, pieces=(), kind=jnp.bfloat16):
    drawn = spread * jax.random.normal(own_key, dims, jnp.float32)
    if pieces:
        drawn = drawn * level_of(own_key, dims, pieces, -0.22, 0.18)
    return jnp.clip(drawn, -bound, bound).astype(kind)


def setup_inputs(seed: int = 0) -> dict:
    key_of = jax.random.split(jax.random.key(seed), 8)
    short_conv_input = centred(key_of[0], (TOKENS, CHANNELS), 1.0, 6.0, ((0, 8), (1, 4)))
    out_gate = centred(key_of[1], (TOKENS, CHANNELS), 1.0, 6.0, ((0, 8), (1, 4)))
    in_gate = centred(key_of[2], (TOKENS, CHANNELS), 1.0, 6.0, ((0, 8), (1, 4)))
    out_cotangent = centred(key_of[3], (TOKENS, CHANNELS), 1.0, 6.0, ((0, 8), (1, 4)))
    mr_filter = centred(key_of[4], (FILTER_TAPS, GROUPS), FILTER_TAPS ** -0.5, 0.5, ((1, 4),))
    residues = centred(key_of[5], (MODES, CHANNELS), 1.0, 5.0, ((1, 32),), jnp.float32)
    rates = jnp.clip(jnp.exp(math.log(0.03) - 3.424914 * jax.random.uniform(key_of[6], (MODES, CHANNELS), jnp.float32) ** level_of(key_of[6], (MODES, CHANNELS), ((1, 32),), -0.2, 0.2)), 0.0009765625, 0.03)
    return dict(short_conv_input=short_conv_input, out_gate=out_gate, in_gate=in_gate, out_cotangent=out_cotangent, mr_filter=mr_filter, residues=residues, rates=rates)


def reference(short_conv_input, out_gate, in_gate, out_cotangent, mr_filter, residues, rates):
    single_float = jnp.float32
    bf16 = jnp.bfloat16
    length = short_conv_input.shape[0]
    xf = short_conv_input.astype(single_float)
    gfull = jnp.repeat(mr_filter.astype(single_float), GROUP, axis=1)
    xpad = jnp.concatenate([jnp.zeros((FILTER_TAPS, short_conv_input.shape[1]), single_float), xf], axis=0)

    def add_tap(j, total):
        segment_part = lax.dynamic_slice_in_dim(xpad, (FILTER_TAPS - j).astype(jnp.int32), length, 0)
        return total + gfull[j][None, :] * segment_part
    v = lax.fori_loop(jnp.int32(0), jnp.int32(FILTER_TAPS), add_tap, jnp.zeros(short_conv_input.shape, single_float)).astype(bf16)
    u = (in_gate.astype(single_float) * v.astype(single_float)).astype(bf16)
    dz = (out_gate.astype(single_float) * out_cotangent.astype(single_float)).astype(bf16)
    norm = jnp.sqrt(2.0 * rates / MODES)
    weights = residues * norm
    tau = jnp.arange(length).astype(single_float)

    def add_mode(total, pair):
        weight, rate = pair
        return (total + weight[None, :] * jnp.exp(-rate[None, :] * tau[:, None]), None)
    h, _ = lax.scan(add_mode, jnp.zeros(short_conv_input.shape, single_float), (weights, rates))
    size = 2 * length
    hf = jnp.fft.rfft(h, n=size, axis=0)
    uf = jnp.fft.rfft(u.astype(single_float), n=size, axis=0)
    df = jnp.fft.rfft(dz.astype(single_float), n=size, axis=0)
    z = jnp.fft.irfft(hf * uf, n=size, axis=0)[:length].astype(bf16)
    du = jnp.fft.irfft(jnp.conj(hf) * df, n=size, axis=0)[:length].astype(bf16)
    dh = jnp.fft.irfft(jnp.conj(uf) * df, n=size, axis=0)[:length]
    out_gate_grad = (out_cotangent.astype(single_float) * z.astype(single_float)).astype(bf16)
    in_gate_grad = (du.astype(single_float) * v.astype(single_float)).astype(bf16)
    value_grad = (du.astype(single_float) * in_gate.astype(single_float)).astype(bf16)
    value_grad_full = value_grad.astype(single_float)
    value_grad_padded = jnp.concatenate([value_grad_full, jnp.zeros((FILTER_TAPS, short_conv_input.shape[1]), single_float)], axis=0)

    def add_back(j, total):
        segment_part = lax.dynamic_slice_in_dim(value_grad_padded, j.astype(jnp.int32), length, 0)
        return total + gfull[j][None, :] * segment_part
    input_grad = lax.fori_loop(jnp.int32(0), jnp.int32(FILTER_TAPS), add_back, jnp.zeros(short_conv_input.shape, single_float)).astype(bf16)
    scale = 1.0 / jnp.sqrt(jnp.asarray(length, single_float))

    def tap_sum(j):
        segment_part = lax.dynamic_slice_in_dim(xpad, (FILTER_TAPS - j).astype(jnp.int32), length, 0)
        channel_wise = lax.optimization_barrier(jnp.sum(value_grad_full * segment_part, axis=0))
        return lax.optimization_barrier(jnp.sum(channel_wise.reshape(-1, GROUP), axis=1))
    filter_grad = lax.map(tap_sum, jnp.arange(FILTER_TAPS, dtype=jnp.int32)) * scale

    def mode_sums(rate):
        decay = jnp.exp(-rate[None, :] * tau[:, None])
        first = lax.optimization_barrier(jnp.sum(dh * decay, axis=0))
        second = lax.optimization_barrier(jnp.sum(dh * decay * tau[:, None], axis=0))
        return (first, second)
    s1, s2 = lax.map(mode_sums, rates)
    residue_grad = norm * s1 * scale
    rate_grad = weights * (0.5 * s1 - rates * s2) * scale
    return (input_grad, out_gate_grad, in_gate_grad, filter_grad, residue_grad, rate_grad)
```

```python
import functools
import math

import jax
import jax.numpy as jnp
import numpy as np
from jax import lax
from jax.experimental import pallas as pl
from jax.experimental.pallas import tpu as pltpu
from jax.sharding import PartitionSpec as P

MESH = pl.DeviceIdType.MESH
F32, BF16 = jnp.float32, jnp.bfloat16
AXIS = "ctx"


def dft_tables(half):
    size = 2 * half
    k = np.arange(half)[:, None]
    t = np.arange(half)[None, :]
    angle = 2.0 * np.pi * (k * t % size) / size
    real, imag = np.cos(angle), -np.sin(angle)
    imag[0] = np.cos(np.pi * np.arange(half))
    forward = np.concatenate([real, imag], axis=0)
    gain = np.full((size, 1), 2.0 / size)
    gain[0] = gain[half] = 1.0 / size
    inverse = (forward * gain).T

    def split(table):
        table = table.astype(np.float32)
        high = table.astype(BF16)
        return high, (table - high.astype(np.float32)).astype(BF16)

    return np.concatenate(split(forward), axis=1), np.concatenate(split(inverse), axis=0)


def dot(left, right):
    return jnp.dot(left, right, preferred_element_type=F32)


def split(value):
    high = value.astype(BF16)
    return high, (value - high.astype(F32)).astype(BF16)


def product(left, right):
    return (left.astype(F32) * right.astype(F32)).astype(BF16)


def kernel(
    n, x_ref, og_ref, ig_ref, oc_ref, filt_ref, res_ref, rate_ref, fwd_ref, inv_ref,
    xg_ref, ogg_ref, igg_ref, fg_ref, rg_ref, tg_ref,
    rim, rr_all, d_all, u_all, dv, dv_rim, mp_send, mp_all, fg_all,
    rates, resid, decay, decay_rev, h_ref, d_sum, u_sum, m_sum, dz_ref, u_ref, g_ref,
    back_ref, conv_ref, xs_ref, fs_ref,
    rim_sem, rr_send, rr_recv, d_send, d_recv, u_send, u_recv, dv_sem, mp_ssem, mp_rsem, fg_send, fg_recv,
):
    me = lax.axis_index(AXIS)
    rows, chans = x_ref.shape
    modes, own = rate_ref.shape
    groups = filt_ref.shape[1]
    parts = modes // 8

    barrier = pltpu.get_barrier_semaphore()

    def greet(k, carry):
        pl.semaphore_signal(barrier, inc=1, device_id={AXIS: lax.rem(me + k, n)}, device_id_type=MESH)
        return carry

    lax.fori_loop(1, n, greet, 0)
    for g in range(parts):
        rr_all[me, :, g * own : (g + 1) * own] = rate_ref[8 * g : 8 * g + 8, :]
        rr_all[me, :, (parts + g) * own : (parts + g + 1) * own] = res_ref[8 * g : 8 * g + 8, :]
    pl.semaphore_wait(barrier, n - 1)

    def remote(src, dst, ssem, rsem, to):
        return pltpu.make_async_remote_copy(
            src_ref=src, dst_ref=dst, send_sem=ssem, recv_sem=rsem, device_id={AXIS: to}, device_id_type=MESH
        )

    def rr_copy(slot, to):
        return remote(rr_all.at[slot], rr_all.at[slot], rr_send.at[to], rr_recv.at[slot], to)

    def fg_copy(slot, to):
        return remote(fg_all.at[slot], fg_all.at[slot], fg_send.at[to], fg_recv.at[slot], to)

    def mp_copy(slot, to):
        return remote(mp_send.at[to], mp_all.at[slot], mp_ssem.at[to], mp_rsem.at[slot], to)

    def d_copy(slot, to):
        return remote(d_all.at[slot], d_all.at[slot], d_send.at[to], d_recv.at[slot], to)

    def u_copy(slot, to):
        return remote(u_all.at[slot], u_all.at[slot], u_send.at[to], u_recv.at[slot], to)

    def rim_copy(to):
        return remote(x_ref, rim, rim_sem.at[0], rim_sem.at[1], to)

    def dv_copy(to):
        return remote(dv, dv_rim, dv_sem.at[0], dv_sem.at[1], to)

    def others(act):
        def step(k, carry):
            act(lax.rem(me + k, n))
            return carry

        lax.fori_loop(1, n, step, 0)

    def span(lo, hi, act):
        def step(j, carry):
            act(j)
            return carry

        lax.fori_loop(lo, hi, step, 0)

    others(lambda j: rr_copy(me, j).start())

    @pl.when(me < n - 1)
    def _():
        rim_copy(me + 1).start()

    fwd = fwd_ref[...]
    fwd_hi = fwd[:, :rows]
    inv_hi = inv_ref[:rows, :]
    inv_lo = inv_ref[rows:, :]
    tau = lax.broadcasted_iota(jnp.int32, (rows, chans), 0)
    first_row = tau == 0
    tau_f = tau.astype(F32)
    left_f = (rows - 1) - tau_f
    sign = (1 - 2 * lax.rem(lax.broadcasted_iota(jnp.int32, (2 * rows, chans), 0), 2)).astype(F32)

    def spectrum(value):
        return dot(fwd, jnp.concatenate([value, value], axis=0))

    def signal(spec):
        high, low = split(spec)
        return dot(inv_hi, high) + dot(inv_hi, low) + dot(inv_lo, high)

    def times(a, b, conj):
        ar, ai, br, bi = a[:rows], a[rows:], b[:rows], b[rows:]
        pure = ai * bi
        cross = jnp.where(first_row, 0.0, pure)
        if conj:
            return jnp.concatenate([ar * br + cross, jnp.where(first_row, pure, ar * bi - ai * br)], axis=0)
        return jnp.concatenate([ar * br - cross, jnp.where(first_row, pure, ar * bi + ai * br)], axis=0)

    member = (
        lax.broadcasted_iota(jnp.int32, (groups, chans), 1) // (chans // groups)
        == lax.broadcasted_iota(jnp.int32, (groups, chans), 0)
    ).astype(BF16)
    taps = dot(filt_ref[...], member).astype(BF16)
    fs_ref[...] = spectrum(taps)
    dz = product(og_ref[...], oc_ref[...])
    dz_ref[...] = dz.astype(F32)
    xs_ref[...] = spectrum(x_ref[...])

    others(lambda j: rr_copy(j, j).wait_recv())
    for j in range(n):
        piece = rr_all[j]
        for g in range(parts):
            rates[8 * g : 8 * g + 8, j * own : (j + 1) * own] = piece[:, g * own : (g + 1) * own]
            resid[8 * g : 8 * g + 8, j * own : (j + 1) * own] = piece[:, (parts + g) * own : (parts + g + 1) * own]

    norm = jnp.sqrt(2.0 * rates[...] / modes)
    resid[...] = resid[...] * norm
    h_ref[...] = jnp.zeros_like(h_ref)

    def build(m, carry):
        rate = rates[pl.ds(m, 1), :]
        e = jnp.exp(-rate * tau_f)
        decay[m] = e
        decay_rev[m] = jnp.exp(-rate * left_f)
        h_ref[...] += resid[pl.ds(m, 1), :] * e
        ed = e * dz_ref[...]
        d_sum[pl.ds(m, 1), :] = jnp.sum(ed, axis=0, keepdims=True)
        d_sum[pl.ds(modes + m, 1), :] = jnp.sum(ed * tau_f, axis=0, keepdims=True)
        return carry

    lax.fori_loop(0, modes, build, 0)
    d_all[me] = d_sum[:modes, :].astype(BF16)
    span(0, me, lambda j: d_copy(me, j).start())

    @pl.when(me == 0)
    def _():
        rim[...] = jnp.zeros_like(rim)

    @pl.when(me > 0)
    def _():
        rim_copy(me).wait_recv()

    xs = xs_ref[...] + sign * spectrum(rim[...])
    xs_ref[...] = xs
    mr = signal(times(fs_ref[...], xs, False)).astype(BF16)
    u = product(ig_ref[...], mr)
    u_ref[...] = u.astype(F32)

    def condense(m, carry):
        eu = decay_rev[m] * u_ref[...]
        u_sum[pl.ds(m, 1), :] = jnp.sum(eu, axis=0, keepdims=True)
        u_sum[pl.ds(modes + m, 1), :] = jnp.sum(eu * left_f, axis=0, keepdims=True)
        return carry

    lax.fori_loop(0, modes, condense, 0)
    u_all[me] = u_sum[...].astype(BF16)
    span(me + 1, n, lambda j: u_copy(me, j).start())

    h_hi, h_lo = split(h_ref[...])
    hs = spectrum(h_hi) + dot(fwd_hi, h_lo)
    us = spectrum(u)
    ds = spectrum(dz)
    back_ref[...] = signal(times(hs, ds, True))
    conv_ref[...] = signal(times(hs, us, False))
    g_ref[...] = signal(times(us, ds, True))

    step_decay = jnp.exp(-rates[...])
    jump = jnp.exp(-rates[...] * rows)

    span(me + 1, n, lambda j: d_copy(j, j).wait_recv())
    later = lax.fori_loop(
        0, n - 1 - me, lambda i, b: b * jump + d_all[n - 1 - i].astype(F32), jnp.zeros((modes, chans), F32)
    )
    m_sum[:modes, :] = resid[...] * step_decay * later

    def spread_back(m, carry):
        back_ref[...] += m_sum[pl.ds(m, 1), :] * decay_rev[m]
        return carry

    lax.fori_loop(0, modes, spread_back, 0)
    back = back_ref[...].astype(BF16)
    grad = product(back, ig_ref[...])
    dv[...] = grad

    @pl.when(me > 0)
    def _():
        dv_copy(me - 1).start()

    dvs = spectrum(grad)
    c_hi, c_lo = split(signal(times(xs_ref[...], dvs, True)))
    nt = (((1,), (1,)), ((), ()))
    fg_all[me] = lax.dot_general(member, c_hi, nt, preferred_element_type=F32) + lax.dot_general(
        member, c_lo, nt, preferred_element_type=F32
    )
    others(lambda j: fg_copy(me, j).start())
    igg_ref[...] = product(back, mr)

    span(0, me, lambda j: u_copy(j, j).wait_recv())

    def prior(j, carry):
        s, s1 = carry
        return (
            s * jump + u_all[j, :modes, :].astype(F32),
            (s1 + rows * s) * jump + u_all[j, modes:, :].astype(F32),
        )

    zero = jnp.zeros((modes, chans), F32)
    s, s1 = lax.fori_loop(0, me, prior, (zero, zero))
    s, s1 = s * step_decay, s1 * step_decay

    def lags(m, carry):
        eg = decay[m] * g_ref[...]
        m_sum[pl.ds(m, 1), :] = jnp.sum(eg, axis=0, keepdims=True)
        m_sum[pl.ds(modes + m, 1), :] = jnp.sum(eg * tau_f, axis=0, keepdims=True)
        return carry

    lax.fori_loop(0, modes, lags, 0)
    d0, d1 = d_sum[:modes, :], d_sum[modes:, :]
    m_sum[:modes, :] += s * d0
    m_sum[modes:, :] += s * (d0 + d1) + s1 * d0
    for j in range(n):
        for g in range(2 * parts):
            mp_send[j, :, g * own : (g + 1) * own] = m_sum[8 * g : 8 * g + 8, j * own : (j + 1) * own]
    mp_all[me] = mp_send[me]
    others(lambda j: mp_copy(me, j).start())

    u_sum[:modes, :] = resid[...] * s

    def spread_conv(m, carry):
        conv_ref[...] += u_sum[pl.ds(m, 1), :] * decay[m]
        return carry

    lax.fori_loop(0, modes, spread_conv, 0)
    ogg_ref[...] = product(oc_ref[...], conv_ref[...].astype(BF16))

    @pl.when(me == n - 1)
    def _():
        dv_rim[...] = jnp.zeros_like(dv_rim)

    @pl.when(me < n - 1)
    def _():
        dv_copy(me).wait_recv()

    ws = dvs + sign * spectrum(dv_rim[...])
    xg_ref[...] = signal(times(fs_ref[...], ws, True)).astype(BF16)

    scale = 1.0 / math.sqrt(rows * n)
    others(lambda j: fg_copy(j, j).wait_recv())
    fg_ref[...] = jnp.sum(fg_all[...], axis=0) * scale
    others(lambda j: mp_copy(j, j).wait_recv())
    total = jnp.sum(mp_all[...], axis=0)
    for g in range(parts):
        rate = rate_ref[8 * g : 8 * g + 8, :]
        gain = jnp.sqrt(2.0 * rate / modes)
        first = total[:, g * own : (g + 1) * own]
        second = total[:, (parts + g) * own : (parts + g + 1) * own]
        rg_ref[8 * g : 8 * g + 8, :] = gain * first * scale
        tg_ref[8 * g : 8 * g + 8, :] = res_ref[8 * g : 8 * g + 8, :] * gain * (0.5 * first - rate * second) * scale

    others(lambda j: rr_copy(me, j).wait_send())
    others(lambda j: fg_copy(me, j).wait_send())
    others(lambda j: mp_copy(me, j).wait_send())
    span(0, me, lambda j: d_copy(me, j).wait_send())
    span(me + 1, n, lambda j: u_copy(me, j).wait_send())

    @pl.when(me < n - 1)
    def _():
        rim_copy(me + 1).wait_send()

    @pl.when(me > 0)
    def _():
        dv_copy(me - 1).wait_send()


def local(x, og, ig, oc, filt, res, rate):
    n = lax.axis_size(AXIS)
    rows, chans = x.shape
    modes, own = rate.shape
    groups = filt.shape[1]
    assert rows == filt.shape[0] and 2 * (modes // 8) * own <= 128 and modes % 8 == 0
    fwd, inv = dft_tables(rows)
    vmem = pl.BlockSpec(memory_space=pltpu.VMEM)
    wide = (rows, chans)
    dma = pltpu.SemaphoreType.DMA
    out = pl.pallas_call(
        functools.partial(kernel, n),
        name="mixer",
        out_shape=(
            jax.ShapeDtypeStruct(wide, BF16),
            jax.ShapeDtypeStruct(wide, BF16),
            jax.ShapeDtypeStruct(wide, BF16),
            jax.ShapeDtypeStruct((groups, rows), F32),
            jax.ShapeDtypeStruct((modes, own), F32),
            jax.ShapeDtypeStruct((modes, own), F32),
        ),
        in_specs=[vmem] * 9,
        out_specs=(vmem,) * 6,
        scratch_shapes=[
            pltpu.VMEM(wide, BF16),
            pltpu.VMEM((n, 8, 128), F32),
            pltpu.VMEM((n, modes, chans), BF16),
            pltpu.VMEM((n, 2 * modes, chans), BF16),
            pltpu.VMEM(wide, BF16),
            pltpu.VMEM(wide, BF16),
            pltpu.VMEM((n, 8, 128), F32),
            pltpu.VMEM((n, 8, 128), F32),
            pltpu.VMEM((n, groups, rows), F32),
            pltpu.VMEM((modes, chans), F32),
            pltpu.VMEM((modes, chans), F32),
            pltpu.VMEM((modes,) + wide, F32),
            pltpu.VMEM((modes,) + wide, F32),
            pltpu.VMEM(wide, F32),
            pltpu.VMEM((2 * modes, chans), F32),
            pltpu.VMEM((2 * modes, chans), F32),
            pltpu.VMEM((2 * modes, chans), F32),
            pltpu.VMEM(wide, F32),
            pltpu.VMEM(wide, F32),
            pltpu.VMEM(wide, F32),
            pltpu.VMEM(wide, F32),
            pltpu.VMEM(wide, F32),
            pltpu.VMEM((2 * rows, chans), F32),
            pltpu.VMEM((2 * rows, chans), F32),
            dma((2,)), dma((n,)), dma((n,)), dma((n,)), dma((n,)), dma((n,)), dma((n,)), dma((2,)),
            dma((n,)), dma((n,)), dma((n,)), dma((n,)),
        ],
        compiler_params=pltpu.CompilerParams(
            collective_id=0, has_side_effects=True, vmem_limit_bytes=32 * 1024 * 1024
        ),
    )(x, og, ig, oc, filt, res, rate, jnp.asarray(fwd), jnp.asarray(inv))
    xg, ogg, igg, fg, rg, tg = out
    return xg, ogg, igg, fg.T, rg, tg


def solution(mesh):
    tokens = P("ctx", "ch")
    shared = P(None, "ch")
    owned = P(None, ("ch", "ctx"))
    return jax.shard_map(
        local,
        mesh=mesh,
        in_specs=(tokens, tokens, tokens, tokens, shared, owned, owned),
        out_specs=(tokens, tokens, tokens, shared, owned, owned),
        check_vma=False,
    )
```

```python
import functools
import math

import jax
import jax.numpy as jnp
import numpy as np
from jax import lax
from jax.experimental import pallas as pl
from jax.experimental.pallas import tpu as pltpu
from jax.sharding import PartitionSpec as P

MESH = pl.DeviceIdType.MESH
F32, BF16 = jnp.float32, jnp.bfloat16
AXIS = "ctx"
GRANT = 60 * 1024 * 1024


def dft_tables(half):
    size = 2 * half
    k = np.arange(half)[:, None]
    t = np.arange(half)[None, :]
    angle = 2.0 * np.pi * (k * t % size) / size
    real, imag = np.cos(angle), -np.sin(angle)
    imag[0] = np.cos(np.pi * np.arange(half))
    forward = np.concatenate([real, imag], axis=0)
    gain = np.full((size, 1), 2.0 / size)
    gain[0] = gain[half] = 1.0 / size
    inverse = (forward * gain).T

    def split(table):
        table = table.astype(np.float32)
        high = table.astype(BF16)
        return high, (table - high.astype(np.float32)).astype(BF16)

    return np.concatenate(split(forward), axis=1), np.concatenate(split(inverse), axis=0)


def dot(left, right):
    return jnp.dot(left, right, preferred_element_type=F32)


def split(value):
    high = value.astype(BF16)
    return high, (value - high.astype(F32)).astype(BF16)


def product(left, right):
    return (left.astype(F32) * right.astype(F32)).astype(BF16)


def kernel(
    n, x_hbm, og_hbm, ig_hbm, oc_hbm, filt_hbm, res_hbm, rate_hbm, fwd_hbm, inv_hbm,
    xg_hbm, ogg_hbm, igg_hbm, fg_hbm, rg_hbm, tg_hbm,
    xg_ref, ogg_ref, igg_ref, fg_ref, rg_ref, tg_ref, out_sem, rim, rr_all, d_all, u_all, dv, dv_rim, mp_send, mp_all, fg_all,
    rates, resid, decay, decay_rev, h_ref, d_sum, u_sum, m_sum, dz_ref, u_ref, g_ref,
    back_ref, conv_ref, xs_ref, fs_ref,
    x_ref, og_ref, ig_ref, oc_ref, filt_ref, res_ref, rate_ref, fwd_ref, inv_ref, in_sem,
    rim_sem, rr_send, rr_recv, d_send, d_recv, u_send, u_recv, dv_sem, mp_ssem, mp_rsem, fg_send, fg_recv,
):
    order = (
        (rate_hbm, rate_ref), (res_hbm, res_ref), (x_hbm, x_ref), (filt_hbm, filt_ref), (fwd_hbm, fwd_ref),
        (og_hbm, og_ref), (oc_hbm, oc_ref), (ig_hbm, ig_ref), (inv_hbm, inv_ref),
    )
    loads = [pltpu.make_async_copy(src, dst, in_sem.at[i]) for i, (src, dst) in enumerate(order)]
    for load in loads:
        load.start()
    finals = (
        (xg_ref, xg_hbm), (ogg_ref, ogg_hbm), (igg_ref, igg_hbm), (fg_ref, fg_hbm), (rg_ref, rg_hbm), (tg_ref, tg_hbm)
    )
    puts = [pltpu.make_async_copy(src, dst, out_sem.at[i]) for i, (src, dst) in enumerate(finals)]
    me = lax.axis_index(AXIS)
    rows, chans = x_ref.shape
    modes, own = rate_ref.shape
    groups = filt_ref.shape[0]
    parts = modes // 8

    barrier = pltpu.get_barrier_semaphore()

    def greet(k, carry):
        pl.semaphore_signal(barrier, inc=1, device_id={AXIS: lax.rem(me + k, n)}, device_id_type=MESH)
        return carry

    lax.fori_loop(1, n, greet, 0)
    loads[0].wait()
    loads[1].wait()
    for g in range(parts):
        rr_all[me, :, g * own : (g + 1) * own] = rate_ref[8 * g : 8 * g + 8, :]
        rr_all[me, :, (parts + g) * own : (parts + g + 1) * own] = res_ref[8 * g : 8 * g + 8, :]
    pl.semaphore_wait(barrier, n - 1)

    def remote(src, dst, ssem, rsem, to):
        return pltpu.make_async_remote_copy(
            src_ref=src, dst_ref=dst, send_sem=ssem, recv_sem=rsem, device_id={AXIS: to}, device_id_type=MESH
        )

    def rr_copy(slot, to):
        return remote(rr_all.at[slot], rr_all.at[slot], rr_send.at[to], rr_recv.at[slot], to)

    def fg_copy(slot, to):
        return remote(fg_all.at[slot], fg_all.at[slot], fg_send.at[to], fg_recv.at[slot], to)

    def mp_copy(slot, to):
        return remote(mp_send.at[to], mp_all.at[slot], mp_ssem.at[to], mp_rsem.at[slot], to)

    def d_copy(slot, to):
        return remote(d_all.at[slot], d_all.at[slot], d_send.at[to], d_recv.at[slot], to)

    def u_copy(slot, to):
        return remote(u_all.at[slot], u_all.at[slot], u_send.at[to], u_recv.at[slot], to)

    def rim_copy(to):
        return remote(x_ref, rim, rim_sem.at[0], rim_sem.at[1], to)

    def dv_copy(to):
        return remote(dv, dv_rim, dv_sem.at[0], dv_sem.at[1], to)

    def others(act):
        def step(k, carry):
            act(lax.rem(me + k, n))
            return carry

        lax.fori_loop(1, n, step, 0)

    def span(lo, hi, act):
        def step(j, carry):
            act(j)
            return carry

        lax.fori_loop(lo, hi, step, 0)

    others(lambda j: rr_copy(me, j).start())
    loads[2].wait()

    @pl.when(me < n - 1)
    def _():
        rim_copy(me + 1).start()

    for load in loads[3:]:
        load.wait()
    fwd = fwd_ref[...]
    fwd_hi = fwd[:, :rows]
    inv_hi = inv_ref[:rows, :]
    inv_lo = inv_ref[rows:, :]
    tau = lax.broadcasted_iota(jnp.int32, (rows, chans), 0)
    first_row = tau == 0
    tau_f = tau.astype(F32)
    left_f = (rows - 1) - tau_f
    sign = (1 - 2 * lax.rem(lax.broadcasted_iota(jnp.int32, (2 * rows, chans), 0), 2)).astype(F32)

    def spectrum(value):
        return dot(fwd, jnp.concatenate([value, value], axis=0))

    def signal(spec):
        high, low = split(spec)
        return dot(inv_hi, high) + dot(inv_hi, low) + dot(inv_lo, high)

    def times(a, b, conj):
        ar, ai, br, bi = a[:rows], a[rows:], b[:rows], b[rows:]
        pure = ai * bi
        cross = jnp.where(first_row, 0.0, pure)
        if conj:
            return jnp.concatenate([ar * br + cross, jnp.where(first_row, pure, ar * bi - ai * br)], axis=0)
        return jnp.concatenate([ar * br - cross, jnp.where(first_row, pure, ar * bi + ai * br)], axis=0)

    member = (
        lax.broadcasted_iota(jnp.int32, (groups, chans), 1) // (chans // groups)
        == lax.broadcasted_iota(jnp.int32, (groups, chans), 0)
    ).astype(BF16)
    taps = lax.dot_general(
        filt_ref[...], member, (((0,), (0,)), ((), ())), preferred_element_type=F32
    ).astype(BF16)
    fs_ref[...] = spectrum(taps)
    dz = product(og_ref[...], oc_ref[...])
    dz_ref[...] = dz.astype(F32)
    xs_ref[...] = spectrum(x_ref[...])

    others(lambda j: rr_copy(j, j).wait_recv())
    for j in range(n):
        piece = rr_all[j]
        for g in range(parts):
            rates[8 * g : 8 * g + 8, j * own : (j + 1) * own] = piece[:, g * own : (g + 1) * own]
            resid[8 * g : 8 * g + 8, j * own : (j + 1) * own] = piece[:, (parts + g) * own : (parts + g + 1) * own]

    norm = jnp.sqrt(2.0 * rates[...] / modes)
    resid[...] = resid[...] * norm
    h_ref[...] = jnp.zeros_like(h_ref)

    def build(m, carry):
        rate = rates[pl.ds(m, 1), :]
        e = jnp.exp(-rate * tau_f)
        decay[m] = e
        decay_rev[m] = jnp.exp(-rate * left_f)
        h_ref[...] += resid[pl.ds(m, 1), :] * e
        ed = e * dz_ref[...]
        d_sum[pl.ds(m, 1), :] = jnp.sum(ed, axis=0, keepdims=True)
        d_sum[pl.ds(modes + m, 1), :] = jnp.sum(ed * tau_f, axis=0, keepdims=True)
        return carry

    lax.fori_loop(0, modes, build, 0)
    d_all[me] = d_sum[:modes, :].astype(BF16)
    span(0, me, lambda j: d_copy(me, j).start())

    @pl.when(me == 0)
    def _():
        rim[...] = jnp.zeros_like(rim)

    @pl.when(me > 0)
    def _():
        rim_copy(me).wait_recv()

    xs = xs_ref[...] + sign * spectrum(rim[...])
    xs_ref[...] = xs
    mr = signal(times(fs_ref[...], xs, False)).astype(BF16)
    u = product(ig_ref[...], mr)
    u_ref[...] = u.astype(F32)

    def condense(m, carry):
        eu = decay_rev[m] * u_ref[...]
        u_sum[pl.ds(m, 1), :] = jnp.sum(eu, axis=0, keepdims=True)
        u_sum[pl.ds(modes + m, 1), :] = jnp.sum(eu * left_f, axis=0, keepdims=True)
        return carry

    lax.fori_loop(0, modes, condense, 0)
    u_all[me] = u_sum[...].astype(BF16)
    span(me + 1, n, lambda j: u_copy(me, j).start())

    h_hi, h_lo = split(h_ref[...])
    hs = spectrum(h_hi) + dot(fwd_hi, h_lo)
    us = spectrum(u)
    ds = spectrum(dz)
    back_ref[...] = signal(times(hs, ds, True))
    conv_ref[...] = signal(times(hs, us, False))
    g_ref[...] = signal(times(us, ds, True))

    step_decay = jnp.exp(-rates[...])
    jump = jnp.exp(-rates[...] * rows)

    span(me + 1, n, lambda j: d_copy(j, j).wait_recv())
    later = lax.fori_loop(
        0, n - 1 - me, lambda i, b: b * jump + d_all[n - 1 - i].astype(F32), jnp.zeros((modes, chans), F32)
    )
    m_sum[:modes, :] = resid[...] * step_decay * later

    def spread_back(m, carry):
        back_ref[...] += m_sum[pl.ds(m, 1), :] * decay_rev[m]
        return carry

    lax.fori_loop(0, modes, spread_back, 0)
    back = back_ref[...].astype(BF16)
    grad = product(back, ig_ref[...])
    dv[...] = grad

    @pl.when(me > 0)
    def _():
        dv_copy(me - 1).start()

    dvs = spectrum(grad)
    c_hi, c_lo = split(signal(times(xs_ref[...], dvs, True)))
    nt = (((1,), (1,)), ((), ()))
    fg_all[me] = lax.dot_general(member, c_hi, nt, preferred_element_type=F32) + lax.dot_general(
        member, c_lo, nt, preferred_element_type=F32
    )
    others(lambda j: fg_copy(me, j).start())
    igg_ref[...] = product(back, mr)
    puts[2].start()

    span(0, me, lambda j: u_copy(j, j).wait_recv())

    def prior(j, carry):
        s, s1 = carry
        return (
            s * jump + u_all[j, :modes, :].astype(F32),
            (s1 + rows * s) * jump + u_all[j, modes:, :].astype(F32),
        )

    zero = jnp.zeros((modes, chans), F32)
    s, s1 = lax.fori_loop(0, me, prior, (zero, zero))
    s, s1 = s * step_decay, s1 * step_decay

    def lags(m, carry):
        eg = decay[m] * g_ref[...]
        m_sum[pl.ds(m, 1), :] = jnp.sum(eg, axis=0, keepdims=True)
        m_sum[pl.ds(modes + m, 1), :] = jnp.sum(eg * tau_f, axis=0, keepdims=True)
        return carry

    lax.fori_loop(0, modes, lags, 0)
    d0, d1 = d_sum[:modes, :], d_sum[modes:, :]
    m_sum[:modes, :] += s * d0
    m_sum[modes:, :] += s * (d0 + d1) + s1 * d0
    for j in range(n):
        for g in range(2 * parts):
            mp_send[j, :, g * own : (g + 1) * own] = m_sum[8 * g : 8 * g + 8, j * own : (j + 1) * own]
    mp_all[me] = mp_send[me]
    others(lambda j: mp_copy(me, j).start())

    u_sum[:modes, :] = resid[...] * s

    def spread_conv(m, carry):
        conv_ref[...] += u_sum[pl.ds(m, 1), :] * decay[m]
        return carry

    lax.fori_loop(0, modes, spread_conv, 0)
    ogg_ref[...] = product(oc_ref[...], conv_ref[...].astype(BF16))
    puts[1].start()

    @pl.when(me == n - 1)
    def _():
        dv_rim[...] = jnp.zeros_like(dv_rim)

    @pl.when(me < n - 1)
    def _():
        dv_copy(me).wait_recv()

    ws = dvs + sign * spectrum(dv_rim[...])
    xg_ref[...] = signal(times(fs_ref[...], ws, True)).astype(BF16)
    puts[0].start()

    scale = 1.0 / math.sqrt(rows * n)
    others(lambda j: fg_copy(j, j).wait_recv())
    fg_ref[...] = jnp.sum(fg_all[...], axis=0) * scale
    puts[3].start()
    others(lambda j: mp_copy(j, j).wait_recv())
    total = jnp.sum(mp_all[...], axis=0)
    for g in range(parts):
        rate = rate_ref[8 * g : 8 * g + 8, :]
        gain = jnp.sqrt(2.0 * rate / modes)
        first = total[:, g * own : (g + 1) * own]
        second = total[:, (parts + g) * own : (parts + g + 1) * own]
        rg_ref[8 * g : 8 * g + 8, :] = gain * first * scale
        tg_ref[8 * g : 8 * g + 8, :] = res_ref[8 * g : 8 * g + 8, :] * gain * (0.5 * first - rate * second) * scale
    puts[4].start()
    puts[5].start()

    others(lambda j: rr_copy(me, j).wait_send())
    others(lambda j: fg_copy(me, j).wait_send())
    others(lambda j: mp_copy(me, j).wait_send())
    span(0, me, lambda j: d_copy(me, j).wait_send())
    span(me + 1, n, lambda j: u_copy(me, j).wait_send())

    @pl.when(me < n - 1)
    def _():
        rim_copy(me + 1).wait_send()

    @pl.when(me > 0)
    def _():
        dv_copy(me - 1).wait_send()

    for put in puts:
        put.wait()


def store(*refs):
    count = (len(refs) - 2) // 3
    sources, targets, holds = refs[:count], refs[count : 2 * count], refs[2 * count : 3 * count]
    takes = [pltpu.make_async_copy(sources[i], holds[i], refs[-2].at[i]) for i in range(count)]
    gives = [pltpu.make_async_copy(holds[i], targets[i], refs[-1].at[i]) for i in range(count)]
    for take in takes:
        take.start()
    for take, give in zip(takes, gives):
        take.wait()
        give.start()
    for give in gives:
        give.wait()


def local(x, og, ig, oc, filt, res, rate):
    n = lax.axis_size(AXIS)
    rows, chans = x.shape
    modes, own = rate.shape
    groups = filt.shape[1]
    assert rows == filt.shape[0] and 2 * (modes // 8) * own <= 128 and modes % 8 == 0
    fwd, inv = dft_tables(rows)
    hbm = pl.BlockSpec(memory_space=pltpu.HBM)
    wide = (rows, chans)
    dma = pltpu.SemaphoreType.DMA
    out = pl.pallas_call(
        functools.partial(kernel, n),
        name="mixer",
        out_shape=(
            jax.ShapeDtypeStruct(wide, BF16),
            jax.ShapeDtypeStruct(wide, BF16),
            jax.ShapeDtypeStruct(wide, BF16),
            jax.ShapeDtypeStruct((groups, rows), F32),
            jax.ShapeDtypeStruct((modes, own), F32),
            jax.ShapeDtypeStruct((modes, own), F32),
        ),
        in_specs=[hbm] * 9,
        out_specs=(hbm,) * 6,
        scratch_shapes=[
            pltpu.VMEM(wide, BF16), pltpu.VMEM(wide, BF16), pltpu.VMEM(wide, BF16), pltpu.VMEM((groups, rows), F32),
            pltpu.VMEM((modes, own), F32), pltpu.VMEM((modes, own), F32), dma((6,)),
            pltpu.VMEM(wide, BF16),
            pltpu.VMEM((n, 8, 128), F32),
            pltpu.VMEM((n, modes, chans), BF16),
            pltpu.VMEM((n, 2 * modes, chans), BF16),
            pltpu.VMEM(wide, BF16),
            pltpu.VMEM(wide, BF16),
            pltpu.VMEM((n, 8, 128), F32),
            pltpu.VMEM((n, 8, 128), F32),
            pltpu.VMEM((n, groups, rows), F32),
            pltpu.VMEM((modes, chans), F32),
            pltpu.VMEM((modes, chans), F32),
            pltpu.VMEM((modes,) + wide, F32),
            pltpu.VMEM((modes,) + wide, F32),
            pltpu.VMEM(wide, F32),
            pltpu.VMEM((2 * modes, chans), F32),
            pltpu.VMEM((2 * modes, chans), F32),
            pltpu.VMEM((2 * modes, chans), F32),
            pltpu.VMEM(wide, F32),
            pltpu.VMEM(wide, F32),
            pltpu.VMEM(wide, F32),
            pltpu.VMEM(wide, F32),
            pltpu.VMEM(wide, F32),
            pltpu.VMEM((2 * rows, chans), F32),
            pltpu.VMEM((2 * rows, chans), F32),
            pltpu.VMEM(wide, BF16), pltpu.VMEM(wide, BF16), pltpu.VMEM(wide, BF16), pltpu.VMEM(wide, BF16),
            pltpu.VMEM((groups, rows), BF16), pltpu.VMEM((modes, own), F32), pltpu.VMEM((modes, own), F32),
            pltpu.VMEM(fwd.shape, BF16), pltpu.VMEM(inv.shape, BF16), dma((9,)),
            dma((2,)), dma((n,)), dma((n,)), dma((n,)), dma((n,)), dma((n,)), dma((n,)), dma((2,)),
            dma((n,)), dma((n,)), dma((n,)), dma((n,)),
        ],
        compiler_params=pltpu.CompilerParams(
            collective_id=0, has_side_effects=True, vmem_limit_bytes=GRANT
        ),
    )(x, og, ig, oc, filt.T, res, rate, jnp.asarray(fwd), jnp.asarray(inv))
    xg, ogg, igg, fg, rg, tg = pl.pallas_call(
        store,
        name="store",
        out_shape=tuple(jax.ShapeDtypeStruct(o.shape, o.dtype) for o in out),
        in_specs=[hbm] * 6,
        out_specs=(hbm,) * 6,
        scratch_shapes=[pltpu.VMEM(o.shape, o.dtype) for o in out] + [dma((6,)), dma((6,))],
        compiler_params=pltpu.CompilerParams(vmem_limit_bytes=GRANT),
    )(*out)
    return xg, ogg, igg, fg.T, rg, tg


def solution(mesh):
    tokens = P("ctx", "ch")
    shared = P(None, "ch")
    owned = P(None, ("ch", "ctx"))
    return jax.shard_map(
        local,
        mesh=mesh,
        in_specs=(tokens, tokens, tokens, tokens, shared, owned, owned),
        out_specs=(tokens, tokens, tokens, shared, owned, owned),
        check_vma=False,
    )
```

```python
import functools
import math

import jax
import jax.numpy as jnp
import numpy as np
from jax import lax
from jax.experimental import pallas as pl
from jax.experimental.pallas import tpu as pltpu
from jax.sharding import PartitionSpec as P

MESH = pl.DeviceIdType.MESH
F32, BF16 = jnp.float32, jnp.bfloat16
AXIS = "ctx"
GRANT = 60 * 1024 * 1024


def dft_tables(half):
    size = 2 * half
    k = np.arange(half)[:, None]
    t = np.arange(half)[None, :]
    angle = 2.0 * np.pi * (k * t % size) / size
    real, imag = np.cos(angle), -np.sin(angle)
    imag[0] = np.cos(np.pi * np.arange(half))
    forward = np.concatenate([real, imag], axis=0)
    gain = np.full((size, 1), 2.0 / size)
    gain[0] = gain[half] = 1.0 / size
    inverse = (forward * gain).T

    def split(table):
        table = table.astype(np.float32)
        high = table.astype(BF16)
        return high, (table - high.astype(np.float32)).astype(BF16)

    return np.concatenate(split(forward), axis=1), np.concatenate(split(inverse), axis=0)


def dot(left, right):
    return jnp.dot(left, right, preferred_element_type=F32)


def split(value):
    high = value.astype(BF16)
    return high, (value - high.astype(F32)).astype(BF16)


def product(left, right):
    return (left.astype(F32) * right.astype(F32)).astype(BF16)


def kernel(
    n, x_hbm, og_hbm, ig_hbm, oc_hbm, filt_hbm, res_hbm, rate_hbm, fwd_hbm, inv_hbm,
    xg_hbm, ogg_hbm, igg_hbm, fg_hbm, rg_hbm, tg_hbm,
    xg_ref, ogg_ref, igg_ref, fg_ref, rg_ref, tg_ref, out_sem, rim, rr_all, d_all, u_all, dv, dv_rim, mp_send, mp_all, fg_all,
    rates, resid, decay, decay_rev, h_ref, d_sum, u_sum, m_sum, dz_ref, u_ref, g_ref,
    back_ref, conv_ref, xs_ref, fs_ref, mr_ref,
    x_ref, og_ref, ig_ref, oc_ref, filt_ref, res_ref, rate_ref, fwd_ref, inv_ref, in_sem,
    rim_sem, rr_send, rr_recv, d_send, d_recv, u_send, u_recv, dv_sem, mp_ssem, mp_rsem, fg_send, fg_recv,
):
    order = (
        (rate_hbm, rate_ref), (res_hbm, res_ref), (x_hbm, x_ref), (filt_hbm, filt_ref), (fwd_hbm, fwd_ref),
        (og_hbm, og_ref), (oc_hbm, oc_ref), (ig_hbm, ig_ref), (inv_hbm, inv_ref),
    )
    loads = [pltpu.make_async_copy(src, dst, in_sem.at[i]) for i, (src, dst) in enumerate(order)]
    for load in loads:
        load.start()
    finals = (
        (xg_ref, xg_hbm), (ogg_ref, ogg_hbm), (igg_ref, igg_hbm), (fg_ref, fg_hbm), (rg_ref, rg_hbm), (tg_ref, tg_hbm)
    )
    puts = [pltpu.make_async_copy(src, dst, out_sem.at[i]) for i, (src, dst) in enumerate(finals)]
    me = lax.axis_index(AXIS)
    rows, chans = x_ref.shape
    modes, own = rate_ref.shape
    groups = filt_ref.shape[0]
    parts = modes // 8

    barrier = pltpu.get_barrier_semaphore()

    def greet(k, carry):
        pl.semaphore_signal(barrier, inc=1, device_id={AXIS: lax.rem(me + k, n)}, device_id_type=MESH)
        return carry

    lax.fori_loop(1, n, greet, 0)
    loads[0].wait()
    loads[1].wait()
    for g in range(parts):
        rr_all[me, :, g * own : (g + 1) * own] = rate_ref[8 * g : 8 * g + 8, :]
        rr_all[me, :, (parts + g) * own : (parts + g + 1) * own] = res_ref[8 * g : 8 * g + 8, :]
    pl.semaphore_wait(barrier, n - 1)

    def remote(src, dst, ssem, rsem, to):
        return pltpu.make_async_remote_copy(
            src_ref=src, dst_ref=dst, send_sem=ssem, recv_sem=rsem, device_id={AXIS: to}, device_id_type=MESH
        )

    def rr_copy(slot, to):
        return remote(rr_all.at[slot], rr_all.at[slot], rr_send.at[to], rr_recv.at[slot], to)

    def fg_copy(slot, to):
        return remote(fg_all.at[slot], fg_all.at[slot], fg_send.at[to], fg_recv.at[slot], to)

    def mp_copy(slot, to):
        return remote(mp_send.at[to], mp_all.at[slot], mp_ssem.at[to], mp_rsem.at[slot], to)

    def d_copy(slot, to):
        return remote(d_all.at[slot], d_all.at[slot], d_send.at[to], d_recv.at[slot], to)

    def u_copy(slot, to):
        return remote(u_all.at[slot], u_all.at[slot], u_send.at[to], u_recv.at[slot], to)

    def rim_copy(to):
        return remote(x_ref, rim, rim_sem.at[0], rim_sem.at[1], to)

    def dv_copy(to):
        return remote(dv, dv_rim, dv_sem.at[0], dv_sem.at[1], to)

    def others(act):
        def step(k, carry):
            act(lax.rem(me + k, n))
            return carry

        lax.fori_loop(1, n, step, 0)

    def span(lo, hi, act):
        def step(j, carry):
            act(j)
            return carry

        lax.fori_loop(lo, hi, step, 0)

    others(lambda j: rr_copy(me, j).start())
    loads[2].wait()

    @pl.when(me < n - 1)
    def _():
        rim_copy(me + 1).start()

    for load in loads[3:]:
        load.wait()
    fwd = fwd_ref[...]
    fwd_hi = fwd[:, :rows]
    inv_hi = inv_ref[:rows, :]
    inv_lo = inv_ref[rows:, :]
    tau = lax.broadcasted_iota(jnp.int32, (rows, chans), 0)
    first_row = tau == 0
    sign = (1 - 2 * lax.rem(lax.broadcasted_iota(jnp.int32, (2 * rows, chans), 0), 2)).astype(F32)

    def spectrum(value):
        return dot(fwd, jnp.concatenate([value, value], axis=0))

    def signal(spec):
        high, low = split(spec)
        return dot(inv_hi, high) + dot(inv_hi, low) + dot(inv_lo, high)

    def times(a, b, conj):
        ar, ai, br, bi = a[:rows], a[rows:], b[:rows], b[rows:]
        pure = ai * bi
        cross = jnp.where(first_row, 0.0, pure)
        if conj:
            return jnp.concatenate([ar * br + cross, jnp.where(first_row, pure, ar * bi - ai * br)], axis=0)
        return jnp.concatenate([ar * br - cross, jnp.where(first_row, pure, ar * bi + ai * br)], axis=0)

    member = (
        lax.broadcasted_iota(jnp.int32, (groups, chans), 1) // (chans // groups)
        == lax.broadcasted_iota(jnp.int32, (groups, chans), 0)
    ).astype(BF16)
    taps = lax.dot_general(
        filt_ref[...], member, (((0,), (0,)), ((), ())), preferred_element_type=F32
    ).astype(BF16)
    fs_ref[...] = spectrum(taps)
    dz = product(og_ref[...], oc_ref[...])
    dz_ref[...] = dz.astype(F32)
    xs_ref[...] = spectrum(x_ref[...])

    others(lambda j: rr_copy(j, j).wait_recv())
    for j in range(n):
        piece = rr_all[j]
        for g in range(parts):
            rates[8 * g : 8 * g + 8, j * own : (j + 1) * own] = piece[:, g * own : (g + 1) * own]
            resid[8 * g : 8 * g + 8, j * own : (j + 1) * own] = piece[:, (parts + g) * own : (parts + g + 1) * own]

    norm = jnp.sqrt(2.0 * rates[...] / modes)
    resid[...] = resid[...] * norm
    tiles = rows // 8
    low = lax.broadcasted_iota(jnp.int32, (8, chans), 0).astype(F32)
    high = 7.0 - low
    batch = 4

    def put_moments(sums, m, first, second):
        sums[pl.ds(m, 1), :] = jnp.sum(first, axis=0, keepdims=True)
        sums[pl.ds(modes + m, 1), :] = jnp.sum(second, axis=0, keepdims=True)

    def build(group, carry):
        for i in range(batch):
            m = group * batch + i
            rate = jnp.broadcast_to(rates[pl.ds(m, 1), :], (8, chans))
            hop = jnp.exp(-8.0 * rate)
            e = jnp.exp(-rate * low)
            e_rev = jnp.exp(-rate * high)
            first = run = jnp.zeros((8, chans), F32)
            for t in range(tiles):
                decay[m, 8 * t : 8 * t + 8, :] = e
                decay_rev[m, rows - 8 * t - 8 : rows - 8 * t, :] = e_rev
                first += e * dz_ref[8 * t : 8 * t + 8, :]
                if t < tiles - 1:
                    run += first
                    e, e_rev = e * hop, e_rev * hop
            put_moments(d_sum, m, first, 8.0 * ((tiles - 1) * first - run) + low * first)
        return carry

    lax.fori_loop(0, modes // batch, build, 0)

    def moments(sums, table, value, back):
        def step(group, carry):
            first = [jnp.zeros((8, chans), F32)] * batch
            run = list(first)
            for t in range(tiles):
                part = value[8 * t : 8 * t + 8, :]
                for i in range(batch):
                    first[i] += table[group * batch + i, 8 * t : 8 * t + 8, :] * part
                    if t < tiles - 1:
                        run[i] += first[i]
            for i in range(batch):
                if back:
                    second = 8.0 * run[i] + high * first[i]
                else:
                    second = 8.0 * ((tiles - 1) * first[i] - run[i]) + low * first[i]
                put_moments(sums, group * batch + i, first[i], second)
            return carry

        lax.fori_loop(0, modes // batch, step, 0)

    def blend(coef, table, at):
        parts = [coef[m : m + 1, :] * table[m, at, :] for m in range(modes)]
        while len(parts) > 1:
            parts = [left + right for left, right in zip(parts[::2], parts[1::2])]
        return parts[0]

    def blocks(act):
        def step(i, carry):
            act(pl.ds(pl.multiple_of(16 * i, 16), 16))
            return carry

        lax.fori_loop(0, rows // 16, step, 0)

    d_all[me] = d_sum[:modes, :].astype(BF16)
    span(0, me, lambda j: d_copy(me, j).start())

    @pl.when(me == 0)
    def _():
        rim[...] = jnp.zeros_like(rim)

    @pl.when(me > 0)
    def _():
        rim_copy(me).wait_recv()

    xs = xs_ref[...] + sign * spectrum(rim[...])
    xs_ref[...] = xs
    mr = signal(times(fs_ref[...], xs, False)).astype(BF16)
    mr_ref[...] = mr
    u = product(ig_ref[...], mr)
    u_ref[...] = u.astype(F32)

    moments(u_sum, decay_rev, u_ref, True)
    u_all[me] = u_sum[...].astype(BF16)
    span(me + 1, n, lambda j: u_copy(me, j).start())

    def fill(at):
        h_ref[at, :] = blend(resid, decay, at)

    blocks(fill)
    h_hi, h_lo = split(h_ref[...])
    hs = spectrum(h_hi) + dot(fwd_hi, h_lo)
    us = spectrum(u)
    ds = spectrum(dz)
    back_ref[...] = signal(times(hs, ds, True))
    conv_ref[...] = signal(times(hs, us, False))
    g_ref[...] = signal(times(us, ds, True))

    step_decay = jnp.exp(-rates[...])
    jump = jnp.exp(-rates[...] * rows)

    span(me + 1, n, lambda j: d_copy(j, j).wait_recv())
    later = lax.fori_loop(
        0, n - 1 - me, lambda i, b: b * jump + d_all[n - 1 - i].astype(F32), jnp.zeros((modes, chans), F32)
    )
    m_sum[:modes, :] = resid[...] * step_decay * later

    def gates(at):
        back = (back_ref[at, :] + blend(m_sum, decay_rev, at)).astype(BF16)
        dv[at, :] = product(back, ig_ref[at, :])
        igg_ref[at, :] = product(back, mr_ref[at, :])

    blocks(gates)

    @pl.when(me > 0)
    def _():
        dv_copy(me - 1).start()

    puts[2].start()
    dvs = spectrum(dv[...])
    c_hi, c_lo = split(signal(times(xs_ref[...], dvs, True)))
    nt = (((1,), (1,)), ((), ()))
    fg_all[me] = lax.dot_general(member, c_hi, nt, preferred_element_type=F32) + lax.dot_general(
        member, c_lo, nt, preferred_element_type=F32
    )
    others(lambda j: fg_copy(me, j).start())

    span(0, me, lambda j: u_copy(j, j).wait_recv())

    def prior(j, carry):
        s, s1 = carry
        return (
            s * jump + u_all[j, :modes, :].astype(F32),
            (s1 + rows * s) * jump + u_all[j, modes:, :].astype(F32),
        )

    zero = jnp.zeros((modes, chans), F32)
    s, s1 = lax.fori_loop(0, me, prior, (zero, zero))
    s, s1 = s * step_decay, s1 * step_decay

    moments(m_sum, decay, g_ref, False)
    d0, d1 = d_sum[:modes, :], d_sum[modes:, :]
    m_sum[:modes, :] += s * d0
    m_sum[modes:, :] += s * (d0 + d1) + s1 * d0
    for j in range(n):
        for g in range(2 * parts):
            mp_send[j, :, g * own : (g + 1) * own] = m_sum[8 * g : 8 * g + 8, j * own : (j + 1) * own]
    mp_all[me] = mp_send[me]
    others(lambda j: mp_copy(me, j).start())

    u_sum[:modes, :] = resid[...] * s

    def emit(at):
        conv = (conv_ref[at, :] + blend(u_sum, decay, at)).astype(BF16)
        ogg_ref[at, :] = product(oc_ref[at, :], conv)

    blocks(emit)
    puts[1].start()

    @pl.when(me == n - 1)
    def _():
        dv_rim[...] = jnp.zeros_like(dv_rim)

    @pl.when(me < n - 1)
    def _():
        dv_copy(me).wait_recv()

    ws = dvs + sign * spectrum(dv_rim[...])
    xg_ref[...] = signal(times(fs_ref[...], ws, True)).astype(BF16)
    puts[0].start()

    scale = 1.0 / math.sqrt(rows * n)
    others(lambda j: fg_copy(j, j).wait_recv())
    fg_ref[...] = jnp.sum(fg_all[...], axis=0) * scale
    puts[3].start()
    others(lambda j: mp_copy(j, j).wait_recv())
    total = jnp.sum(mp_all[...], axis=0)
    for g in range(parts):
        rate = rate_ref[8 * g : 8 * g + 8, :]
        gain = jnp.sqrt(2.0 * rate / modes)
        first = total[:, g * own : (g + 1) * own]
        second = total[:, (parts + g) * own : (parts + g + 1) * own]
        rg_ref[8 * g : 8 * g + 8, :] = gain * first * scale
        tg_ref[8 * g : 8 * g + 8, :] = res_ref[8 * g : 8 * g + 8, :] * gain * (0.5 * first - rate * second) * scale
    puts[4].start()
    puts[5].start()

    others(lambda j: rr_copy(me, j).wait_send())
    others(lambda j: fg_copy(me, j).wait_send())
    others(lambda j: mp_copy(me, j).wait_send())
    span(0, me, lambda j: d_copy(me, j).wait_send())
    span(me + 1, n, lambda j: u_copy(me, j).wait_send())

    @pl.when(me < n - 1)
    def _():
        rim_copy(me + 1).wait_send()

    @pl.when(me > 0)
    def _():
        dv_copy(me - 1).wait_send()

    for put in puts:
        put.wait()


def store(*refs):
    count = (len(refs) - 2) // 3
    sources, targets, holds = refs[:count], refs[count : 2 * count], refs[2 * count : 3 * count]
    takes = [pltpu.make_async_copy(sources[i], holds[i], refs[-2].at[i]) for i in range(count)]
    gives = [pltpu.make_async_copy(holds[i], targets[i], refs[-1].at[i]) for i in range(count)]
    for take in takes:
        take.start()
    for take, give in zip(takes, gives):
        take.wait()
        give.start()
    for give in gives:
        give.wait()


def local(x, og, ig, oc, filt, res, rate):
    n = lax.axis_size(AXIS)
    rows, chans = x.shape
    modes, own = rate.shape
    groups = filt.shape[1]
    assert rows == filt.shape[0] and modes & (modes - 1) == 0 and 2 * (modes // 8) * own <= 128 and modes % 8 == 0
    fwd, inv = dft_tables(rows)
    hbm = pl.BlockSpec(memory_space=pltpu.HBM)
    wide = (rows, chans)
    dma = pltpu.SemaphoreType.DMA
    out = pl.pallas_call(
        functools.partial(kernel, n),
        name="mixer",
        out_shape=(
            jax.ShapeDtypeStruct(wide, BF16),
            jax.ShapeDtypeStruct(wide, BF16),
            jax.ShapeDtypeStruct(wide, BF16),
            jax.ShapeDtypeStruct((groups, rows), F32),
            jax.ShapeDtypeStruct((modes, own), F32),
            jax.ShapeDtypeStruct((modes, own), F32),
        ),
        in_specs=[hbm] * 9,
        out_specs=(hbm,) * 6,
        scratch_shapes=[
            pltpu.VMEM(wide, BF16), pltpu.VMEM(wide, BF16), pltpu.VMEM(wide, BF16), pltpu.VMEM((groups, rows), F32),
            pltpu.VMEM((modes, own), F32), pltpu.VMEM((modes, own), F32), dma((6,)),
            pltpu.VMEM(wide, BF16),
            pltpu.VMEM((n, 8, 128), F32),
            pltpu.VMEM((n, modes, chans), BF16),
            pltpu.VMEM((n, 2 * modes, chans), BF16),
            pltpu.VMEM(wide, BF16),
            pltpu.VMEM(wide, BF16),
            pltpu.VMEM((n, 8, 128), F32),
            pltpu.VMEM((n, 8, 128), F32),
            pltpu.VMEM((n, groups, rows), F32),
            pltpu.VMEM((modes, chans), F32),
            pltpu.VMEM((modes, chans), F32),
            pltpu.VMEM((modes,) + wide, F32),
            pltpu.VMEM((modes,) + wide, F32),
            pltpu.VMEM(wide, F32),
            pltpu.VMEM((2 * modes, chans), F32),
            pltpu.VMEM((2 * modes, chans), F32),
            pltpu.VMEM((2 * modes, chans), F32),
            pltpu.VMEM(wide, F32),
            pltpu.VMEM(wide, F32),
            pltpu.VMEM(wide, F32),
            pltpu.VMEM(wide, F32),
            pltpu.VMEM(wide, F32),
            pltpu.VMEM((2 * rows, chans), F32),
            pltpu.VMEM((2 * rows, chans), F32),
            pltpu.VMEM(wide, BF16),
            pltpu.VMEM(wide, BF16), pltpu.VMEM(wide, BF16), pltpu.VMEM(wide, BF16), pltpu.VMEM(wide, BF16),
            pltpu.VMEM((groups, rows), BF16), pltpu.VMEM((modes, own), F32), pltpu.VMEM((modes, own), F32),
            pltpu.VMEM(fwd.shape, BF16), pltpu.VMEM(inv.shape, BF16), dma((9,)),
            dma((2,)), dma((n,)), dma((n,)), dma((n,)), dma((n,)), dma((n,)), dma((n,)), dma((2,)),
            dma((n,)), dma((n,)), dma((n,)), dma((n,)),
        ],
        compiler_params=pltpu.CompilerParams(
            collective_id=0, has_side_effects=True, vmem_limit_bytes=GRANT
        ),
    )(x, og, ig, oc, filt.T, res, rate, jnp.asarray(fwd), jnp.asarray(inv))
    xg, ogg, igg, fg, rg, tg = pl.pallas_call(
        store,
        name="store",
        out_shape=tuple(jax.ShapeDtypeStruct(o.shape, o.dtype) for o in out),
        in_specs=[hbm] * 6,
        out_specs=(hbm,) * 6,
        scratch_shapes=[pltpu.VMEM(o.shape, o.dtype) for o in out] + [dma((6,)), dma((6,))],
        compiler_params=pltpu.CompilerParams(vmem_limit_bytes=GRANT),
    )(*out)
    return xg, ogg, igg, fg.T, rg, tg


def solution(mesh):
    tokens = P("ctx", "ch")
    shared = P(None, "ch")
    owned = P(None, ("ch", "ctx"))
    return jax.shard_map(
        local,
        mesh=mesh,
        in_specs=(tokens, tokens, tokens, tokens, shared, owned, owned),
        out_specs=(tokens, tokens, tokens, shared, owned, owned),
        check_vma=False,
    )
```

```python
import functools
import math

import jax
import jax.numpy as jnp
import numpy as np
from jax import lax
from jax.experimental import pallas as pl
from jax.experimental.pallas import tpu as pltpu
from jax.sharding import PartitionSpec as P

MESH = pl.DeviceIdType.MESH
F32, BF16 = jnp.float32, jnp.bfloat16
AXIS = "ctx"
GRANT = 60 * 1024 * 1024


def dft_tables(half):
    size = 2 * half
    k = np.arange(half)[:, None]
    t = np.arange(half)[None, :]
    angle = 2.0 * np.pi * (k * t % size) / size
    real, imag = np.cos(angle), -np.sin(angle)
    imag[0] = np.cos(np.pi * np.arange(half))
    forward = np.concatenate([real, imag], axis=0)
    gain = np.full((size, 1), 2.0 / size)
    gain[0] = gain[half] = 1.0 / size
    inverse = (forward * gain).T

    def split(table):
        table = table.astype(np.float32)
        high = table.astype(BF16)
        return high, (table - high.astype(np.float32)).astype(BF16)

    return np.concatenate(split(forward), axis=1), np.concatenate(split(inverse), axis=0)


def dot(left, right):
    return jnp.dot(left, right, preferred_element_type=F32)


def split(value):
    high = value.astype(BF16)
    return high, (value - high.astype(F32)).astype(BF16)


def product(left, right):
    return (left.astype(F32) * right.astype(F32)).astype(BF16)


def kernel(
    n, x_hbm, og_hbm, ig_hbm, oc_hbm, filt_hbm, res_hbm, rate_hbm, fwd_hbm, inv_hbm,
    xg_hbm, ogg_hbm, igg_hbm, fg_hbm, rg_hbm, tg_hbm,
    xg_ref, ogg_ref, igg_ref, fg_ref, rg_ref, tg_ref, out_sem, rim, rr_all, d_all, u_all, dv, dv_rim, mp_send, mp_all, fg_all,
    rates, resid, decay, decay_rev, coef, h_ref, d_sum, u_sum, m_sum, dz_ref, u_ref, g_ref,
    back_ref, conv_ref, xs_ref, fs_ref, mr_ref,
    x_ref, og_ref, ig_ref, oc_ref, filt_ref, res_ref, rate_ref, fwd_ref, inv_ref, in_sem,
    rim_sem, rr_send, rr_recv, d_send, d_recv, u_send, u_recv, dv_sem, mp_ssem, mp_rsem, fg_send, fg_recv,
):
    order = (
        (rate_hbm, rate_ref), (res_hbm, res_ref), (x_hbm, x_ref), (filt_hbm, filt_ref), (fwd_hbm, fwd_ref),
        (og_hbm, og_ref), (oc_hbm, oc_ref), (ig_hbm, ig_ref), (inv_hbm, inv_ref),
    )
    loads = [pltpu.make_async_copy(src, dst, in_sem.at[i]) for i, (src, dst) in enumerate(order)]
    for load in loads:
        load.start()
    finals = (
        (xg_ref, xg_hbm), (ogg_ref, ogg_hbm), (igg_ref, igg_hbm), (fg_ref, fg_hbm), (rg_ref, rg_hbm), (tg_ref, tg_hbm)
    )
    puts = [pltpu.make_async_copy(src, dst, out_sem.at[i]) for i, (src, dst) in enumerate(finals)]
    me = lax.axis_index(AXIS)
    rows, chans = x_ref.shape
    modes, own = rate_ref.shape
    groups = filt_ref.shape[0]
    parts = modes // 8

    barrier = pltpu.get_barrier_semaphore()

    def greet(k, carry):
        pl.semaphore_signal(barrier, inc=1, device_id={AXIS: lax.rem(me + k, n)}, device_id_type=MESH)
        return carry

    lax.fori_loop(1, n, greet, 0)
    loads[0].wait()
    loads[1].wait()
    for g in range(parts):
        rr_all[me, :, g * own : (g + 1) * own] = rate_ref[8 * g : 8 * g + 8, :]
        rr_all[me, :, (parts + g) * own : (parts + g + 1) * own] = res_ref[8 * g : 8 * g + 8, :]
    pl.semaphore_wait(barrier, n - 1)

    def remote(src, dst, ssem, rsem, to):
        return pltpu.make_async_remote_copy(
            src_ref=src, dst_ref=dst, send_sem=ssem, recv_sem=rsem, device_id={AXIS: to}, device_id_type=MESH
        )

    def rr_copy(slot, to):
        return remote(rr_all.at[slot], rr_all.at[slot], rr_send.at[to], rr_recv.at[slot], to)

    def fg_copy(slot, to):
        return remote(fg_all.at[slot], fg_all.at[slot], fg_send.at[to], fg_recv.at[slot], to)

    def mp_copy(slot, to):
        return remote(mp_send.at[to], mp_all.at[slot], mp_ssem.at[to], mp_rsem.at[slot], to)

    def d_copy(slot, to):
        return remote(d_all.at[slot], d_all.at[slot], d_send.at[to], d_recv.at[slot], to)

    def u_copy(slot, to):
        return remote(u_all.at[slot], u_all.at[slot], u_send.at[to], u_recv.at[slot], to)

    def rim_copy(to):
        return remote(x_ref, rim, rim_sem.at[0], rim_sem.at[1], to)

    def dv_copy(to):
        return remote(dv, dv_rim, dv_sem.at[0], dv_sem.at[1], to)

    def others(act):
        def step(k, carry):
            act(lax.rem(me + k, n))
            return carry

        lax.fori_loop(1, n, step, 0)

    def span(lo, hi, act):
        def step(j, carry):
            act(j)
            return carry

        lax.fori_loop(lo, hi, step, 0)

    others(lambda j: rr_copy(me, j).start())
    loads[2].wait()

    @pl.when(me < n - 1)
    def _():
        rim_copy(me + 1).start()

    for load in loads[3:]:
        load.wait()
    fwd = fwd_ref[...]
    fwd_hi = fwd[:, :rows]
    inv_hi = inv_ref[:rows, :]
    inv_lo = inv_ref[rows:, :]
    tau = lax.broadcasted_iota(jnp.int32, (rows, chans), 0)
    first_row = tau == 0
    sign = (1 - 2 * lax.rem(lax.broadcasted_iota(jnp.int32, (2 * rows, chans), 0), 2)).astype(F32)

    def spectrum(value):
        return dot(fwd, jnp.concatenate([value, value], axis=0))

    def signal(spec):
        high, low = split(spec)
        return dot(inv_hi, high) + dot(inv_hi, low) + dot(inv_lo, high)

    def times(a, b, conj):
        ar, ai, br, bi = a[:rows], a[rows:], b[:rows], b[rows:]
        pure = ai * bi
        cross = jnp.where(first_row, 0.0, pure)
        if conj:
            return jnp.concatenate([ar * br + cross, jnp.where(first_row, pure, ar * bi - ai * br)], axis=0)
        return jnp.concatenate([ar * br - cross, jnp.where(first_row, pure, ar * bi + ai * br)], axis=0)

    member = (
        lax.broadcasted_iota(jnp.int32, (groups, chans), 1) // (chans // groups)
        == lax.broadcasted_iota(jnp.int32, (groups, chans), 0)
    ).astype(BF16)
    taps = lax.dot_general(
        filt_ref[...], member, (((0,), (0,)), ((), ())), preferred_element_type=F32
    ).astype(BF16)
    fs_ref[...] = spectrum(taps)
    dz = product(og_ref[...], oc_ref[...])
    dz_ref[...] = dz.astype(F32)
    xs_ref[...] = spectrum(x_ref[...])

    others(lambda j: rr_copy(j, j).wait_recv())
    for j in range(n):
        piece = rr_all[j]
        for g in range(parts):
            rates[8 * g : 8 * g + 8, j * own : (j + 1) * own] = piece[:, g * own : (g + 1) * own]
            resid[8 * g : 8 * g + 8, j * own : (j + 1) * own] = piece[:, (parts + g) * own : (parts + g + 1) * own]

    norm = jnp.sqrt(2.0 * rates[...] / modes)
    resid[...] = resid[...] * norm
    tiles = rows // 8
    low = lax.broadcasted_iota(jnp.int32, (8, chans), 0).astype(F32)
    high = 7.0 - low
    batch = 4

    def put_moments(sums, m, first, second):
        sums[pl.ds(m, 1), :] = jnp.sum(first, axis=0, keepdims=True)
        sums[pl.ds(modes + m, 1), :] = jnp.sum(second, axis=0, keepdims=True)

    def build(group, carry):
        for i in range(batch):
            m = group * batch + i
            rate = jnp.broadcast_to(rates[pl.ds(m, 1), :], (8, chans))
            hop = jnp.exp(-8.0 * rate)
            e = jnp.exp(-rate * low)
            e_rev = jnp.exp(-rate * high)
            first = run = jnp.zeros((8, chans), F32)
            for t in range(tiles):
                decay[m, 8 * t : 8 * t + 8, :] = e
                decay_rev[m, rows - 8 * t - 8 : rows - 8 * t, :] = e_rev
                first += e * dz_ref[8 * t : 8 * t + 8, :]
                if t < tiles - 1:
                    run += first
                    e, e_rev = e * hop, e_rev * hop
            put_moments(d_sum, m, first, 8.0 * ((tiles - 1) * first - run) + low * first)
        return carry

    lax.fori_loop(0, modes // batch, build, 0)

    def moments(sums, table, value, back):
        def step(group, carry):
            first = [jnp.zeros((8, chans), F32)] * batch
            run = list(first)
            for t in range(tiles):
                part = value[8 * t : 8 * t + 8, :]
                for i in range(batch):
                    first[i] += table[group * batch + i, 8 * t : 8 * t + 8, :] * part
                    if t < tiles - 1:
                        run[i] += first[i]
            for i in range(batch):
                if back:
                    second = 8.0 * run[i] + high * first[i]
                else:
                    second = 8.0 * ((tiles - 1) * first[i] - run[i]) + low * first[i]
                put_moments(sums, group * batch + i, first[i], second)
            return carry

        lax.fori_loop(0, modes // batch, step, 0)

    def blend(weight, table, at):
        parts = [weight[m : m + 1, :] * table[m, at, :] for m in range(modes)]
        while len(parts) > 1:
            parts = [left + right for left, right in zip(parts[::2], parts[1::2])]
        return parts[0]

    def blocks(act):
        def step(i, carry):
            act(pl.ds(pl.multiple_of(16 * i, 16), 16))
            return carry

        lax.fori_loop(0, rows // 16, step, 0)

    d_all[me] = d_sum[:modes, :].astype(BF16)
    span(0, me, lambda j: d_copy(me, j).start())

    @pl.when(me == 0)
    def _():
        rim[...] = jnp.zeros_like(rim)

    @pl.when(me > 0)
    def _():
        rim_copy(me).wait_recv()

    xs = xs_ref[...] + sign * spectrum(rim[...])
    xs_ref[...] = xs
    mr = signal(times(fs_ref[...], xs, False)).astype(BF16)
    mr_ref[...] = mr
    u = product(ig_ref[...], mr)
    u_ref[...] = u.astype(F32)

    moments(u_sum, decay_rev, u_ref, True)
    u_all[me] = u_sum[:modes, :].astype(BF16)
    span(me + 1, n, lambda j: u_copy(me, j).start())

    def fill(at):
        h_ref[at, :] = blend(resid, decay, at)

    blocks(fill)
    h_hi, h_lo = split(h_ref[...])
    hs = spectrum(h_hi) + dot(fwd_hi, h_lo)
    us = spectrum(u)
    ds = spectrum(dz)
    back_ref[...] = signal(times(hs, ds, True))
    g_ref[...] = signal(times(us, ds, True))
    moments(m_sum, decay, g_ref, False)

    step_decay = jnp.exp(-rates[...])
    jump = jnp.exp(-rates[...] * rows)

    span(me + 1, n, lambda j: d_copy(j, j).wait_recv())
    later = lax.fori_loop(
        0, n - 1 - me, lambda i, b: b * jump + d_all[n - 1 - i].astype(F32), jnp.zeros((modes, chans), F32)
    )
    coef[...] = resid[...] * step_decay * later

    def gates(at):
        back = (back_ref[at, :] + blend(coef, decay_rev, at)).astype(BF16)
        dv[at, :] = product(back, ig_ref[at, :])
        igg_ref[at, :] = product(back, mr_ref[at, :])

    blocks(gates)

    @pl.when(me > 0)
    def _():
        dv_copy(me - 1).start()

    puts[2].start()
    dvs = spectrum(dv[...])
    c_hi, c_lo = split(signal(times(xs_ref[...], dvs, True)))
    nt = (((1,), (1,)), ((), ()))
    fg_all[me] = (
        lax.dot_general(member, c_hi, nt, preferred_element_type=F32)
        + lax.dot_general(member, c_lo, nt, preferred_element_type=F32)
    ).astype(BF16)
    others(lambda j: fg_copy(me, j).start())

    conv_ref[...] = signal(times(hs, us, False))
    span(0, me, lambda j: u_copy(j, j).wait_recv())

    def prior(j, carry):
        s, far = carry
        return s * jump + u_all[j].astype(F32), (far + s) * jump

    zero = jnp.zeros((modes, chans), F32)
    s, far = lax.fori_loop(0, me, prior, (zero, zero))
    s = s * step_decay
    d0, d1 = d_sum[:modes, :], d_sum[modes:, :]
    m_sum[:modes, :] += s * d0
    m_sum[modes:, :] += s * (d0 + d1) + step_decay * (rows * far * d0 + u_sum[modes:, :] * later)
    for j in range(n):
        for g in range(2 * parts):
            mp_send[j, :, g * own : (g + 1) * own] = m_sum[8 * g : 8 * g + 8, j * own : (j + 1) * own]
    mp_all[me] = mp_send[me]
    others(lambda j: mp_copy(me, j).start())

    coef[...] = resid[...] * s

    def emit(at):
        conv = (conv_ref[at, :] + blend(coef, decay, at)).astype(BF16)
        ogg_ref[at, :] = product(oc_ref[at, :], conv)

    blocks(emit)
    puts[1].start()

    @pl.when(me == n - 1)
    def _():
        dv_rim[...] = jnp.zeros_like(dv_rim)

    @pl.when(me < n - 1)
    def _():
        dv_copy(me).wait_recv()

    ws = dvs + sign * spectrum(dv_rim[...])
    xg_ref[...] = signal(times(fs_ref[...], ws, True)).astype(BF16)
    puts[0].start()

    scale = 1.0 / math.sqrt(rows * n)
    others(lambda j: fg_copy(j, j).wait_recv())
    fg_ref[...] = jnp.sum(fg_all[...].astype(F32), axis=0) * scale
    puts[3].start()
    others(lambda j: mp_copy(j, j).wait_recv())
    total = jnp.sum(mp_all[...], axis=0)
    for g in range(parts):
        rate = rate_ref[8 * g : 8 * g + 8, :]
        gain = jnp.sqrt(2.0 * rate / modes)
        first = total[:, g * own : (g + 1) * own]
        second = total[:, (parts + g) * own : (parts + g + 1) * own]
        rg_ref[8 * g : 8 * g + 8, :] = gain * first * scale
        tg_ref[8 * g : 8 * g + 8, :] = res_ref[8 * g : 8 * g + 8, :] * gain * (0.5 * first - rate * second) * scale
    puts[4].start()
    puts[5].start()

    others(lambda j: rr_copy(me, j).wait_send())
    others(lambda j: fg_copy(me, j).wait_send())
    others(lambda j: mp_copy(me, j).wait_send())
    span(0, me, lambda j: d_copy(me, j).wait_send())
    span(me + 1, n, lambda j: u_copy(me, j).wait_send())

    @pl.when(me < n - 1)
    def _():
        rim_copy(me + 1).wait_send()

    @pl.when(me > 0)
    def _():
        dv_copy(me - 1).wait_send()

    for put in puts:
        put.wait()


def store(*refs):
    count = (len(refs) - 2) // 3
    sources, targets, holds = refs[:count], refs[count : 2 * count], refs[2 * count : 3 * count]
    takes = [pltpu.make_async_copy(sources[i], holds[i], refs[-2].at[i]) for i in range(count)]
    gives = [pltpu.make_async_copy(holds[i], targets[i], refs[-1].at[i]) for i in range(count)]
    for take in takes:
        take.start()
    for take, give in zip(takes, gives):
        take.wait()
        give.start()
    for give in gives:
        give.wait()


def local(x, og, ig, oc, filt, res, rate):
    n = lax.axis_size(AXIS)
    rows, chans = x.shape
    modes, own = rate.shape
    groups = filt.shape[1]
    assert rows == filt.shape[0] and modes & (modes - 1) == 0 and 2 * (modes // 8) * own <= 128 and modes % 8 == 0
    fwd, inv = dft_tables(rows)
    hbm = pl.BlockSpec(memory_space=pltpu.HBM)
    wide = (rows, chans)
    dma = pltpu.SemaphoreType.DMA
    out = pl.pallas_call(
        functools.partial(kernel, n),
        name="mixer",
        out_shape=(
            jax.ShapeDtypeStruct(wide, BF16),
            jax.ShapeDtypeStruct(wide, BF16),
            jax.ShapeDtypeStruct(wide, BF16),
            jax.ShapeDtypeStruct((groups, rows), F32),
            jax.ShapeDtypeStruct((modes, own), F32),
            jax.ShapeDtypeStruct((modes, own), F32),
        ),
        in_specs=[hbm] * 9,
        out_specs=(hbm,) * 6,
        scratch_shapes=[
            pltpu.VMEM(wide, BF16), pltpu.VMEM(wide, BF16), pltpu.VMEM(wide, BF16), pltpu.VMEM((groups, rows), F32),
            pltpu.VMEM((modes, own), F32), pltpu.VMEM((modes, own), F32), dma((6,)),
            pltpu.VMEM(wide, BF16),
            pltpu.VMEM((n, 8, 128), F32),
            pltpu.VMEM((n, modes, chans), BF16),
            pltpu.VMEM((n, modes, chans), BF16),
            pltpu.VMEM(wide, BF16),
            pltpu.VMEM(wide, BF16),
            pltpu.VMEM((n, 8, 128), F32),
            pltpu.VMEM((n, 8, 128), F32),
            pltpu.VMEM((n, groups, rows), BF16),
            pltpu.VMEM((modes, chans), F32),
            pltpu.VMEM((modes, chans), F32),
            pltpu.VMEM((modes,) + wide, F32),
            pltpu.VMEM((modes,) + wide, F32),
            pltpu.VMEM((modes, chans), F32),
            pltpu.VMEM(wide, F32),
            pltpu.VMEM((2 * modes, chans), F32),
            pltpu.VMEM((2 * modes, chans), F32),
            pltpu.VMEM((2 * modes, chans), F32),
            pltpu.VMEM(wide, F32),
            pltpu.VMEM(wide, F32),
            pltpu.VMEM(wide, F32),
            pltpu.VMEM(wide, F32),
            pltpu.VMEM(wide, F32),
            pltpu.VMEM((2 * rows, chans), F32),
            pltpu.VMEM((2 * rows, chans), F32),
            pltpu.VMEM(wide, BF16),
            pltpu.VMEM(wide, BF16), pltpu.VMEM(wide, BF16), pltpu.VMEM(wide, BF16), pltpu.VMEM(wide, BF16),
            pltpu.VMEM((groups, rows), BF16), pltpu.VMEM((modes, own), F32), pltpu.VMEM((modes, own), F32),
            pltpu.VMEM(fwd.shape, BF16), pltpu.VMEM(inv.shape, BF16), dma((9,)),
            dma((2,)), dma((n,)), dma((n,)), dma((n,)), dma((n,)), dma((n,)), dma((n,)), dma((2,)),
            dma((n,)), dma((n,)), dma((n,)), dma((n,)),
        ],
        compiler_params=pltpu.CompilerParams(
            collective_id=0, has_side_effects=True, vmem_limit_bytes=GRANT
        ),
    )(x, og, ig, oc, filt.T, res, rate, jnp.asarray(fwd), jnp.asarray(inv))
    xg, ogg, igg, fg, rg, tg = pl.pallas_call(
        store,
        name="store",
        out_shape=tuple(jax.ShapeDtypeStruct(o.shape, o.dtype) for o in out),
        in_specs=[hbm] * 6,
        out_specs=(hbm,) * 6,
        scratch_shapes=[pltpu.VMEM(o.shape, o.dtype) for o in out] + [dma((6,)), dma((6,))],
        compiler_params=pltpu.CompilerParams(vmem_limit_bytes=GRANT),
    )(*out)
    return xg, ogg, igg, fg.T, rg, tg


def solution(mesh):
    tokens = P("ctx", "ch")
    shared = P(None, "ch")
    owned = P(None, ("ch", "ctx"))
    return jax.shard_map(
        local,
        mesh=mesh,
        in_specs=(tokens, tokens, tokens, tokens, shared, owned, owned),
        out_specs=(tokens, tokens, tokens, shared, owned, owned),
        check_vma=False,
    )
```
